32 devices in a mesh: group: 2 (over x), ctx: 16 (over z, y, core).
Axes of the slice: x: 2, y: 2, z: 4, core: 2. Of those that a mesh axis runs over, the one named last changes fastest.
Arguments:
- query_rows: bfloat16 [4096, 4096], P(('group', 'ctx')), parts along dimension 0, may hold values from -6 to 6
- key_rows: bfloat16 [4096, 4096], P(('group', 'ctx')), parts along dimension 0, may hold values from -6 to 6
- value_rows: bfloat16 [4096, 4096], P(('group', 'ctx')), parts along dimension 0, may hold values from -6 to 6
- conv_taps: float32 [3, 3, 4096], replicated, may hold values from -3.5 to 3.5
- decay_rate: float32 [4096], replicated, may hold values from 0.0007324219 to 0.034
- lag_profile: float32 [2048], replicated, may hold values from -3.6681164 to 3.6681164
- skip_gain: float32 [4096], replicated, may hold values from 0.5 to 1.5
- pair_lists: int32 [32, 9, 2], P('group'), parts along dimension 0, may hold values from -1 to 15, as said below
Outputs:
- layer_out: bfloat16 [4096, 4096], P(('group', 'ctx')), parts along dimension 0
The draws below stay inside these ranges and needn't reach their ends.
There are 2 independent parts, one for each index of `group`. The reference program is written for one: setup_inputs(seed, part) draws one part's arguments, and reference() takes and returns one part's arrays. A program takes and returns all parts, laid end to end along the dimension named above; an argument that names none is the same for every part. Nothing has to cross between parts.
Inputs may be any that keep to these rules, and one draw needn't show every extreme that they name: `pair_lists`: row r lists the pairs that reader r handles. Every live pair (source span <= target span, both in the same document) appears exactly once over all rows, and no other pair appears. A reader's sources are r or 15 - r, its targets are distinct, and unused entries are (-1, -1) after the used ones; some reader's row is full. The sequence holds two documents, the second beginning at a span between 4 and 12.
All inputs are finite; a program needn't handle non-finite values.
Results may differ from the reference program's by a relative error of at most 0.0051.
Values may be sent and summed in bfloat16 or wider, within the bound.
A program may use at most 128 MiB of HBM per device.

```python
import jax
import jax.numpy as jnp
from jax import lax

D = 4096
TOK_DEV = 128
SEQ = 2048
SLOTS = 9
N_CTX = 16


def document_of(span_ids, border):
    return (span_ids >= border).astype(jnp.int32)


def draw_pair_lists(key, part):
    border = jax.random.randint(jax.random.fold_in(key, 7), (), N_CTX // 4, 3 * N_CTX // 4 + 1)
    half_count = N_CTX // 2
    readers = jnp.arange(N_CTX, dtype=jnp.int32)[:, None]
    targets = jnp.arange(N_CTX, dtype=jnp.int32)[None, :]
    lower = jnp.where(readers < half_count, readers, N_CTX - 1 - readers)
    upper = N_CTX - 1 - lower
    source = jnp.where((readers < half_count) & (targets >= half_count), upper, lower)
    reach_from = jnp.where(readers < half_count, jnp.where(targets < half_count, lower, upper), half_count)
    valid = (targets >= reach_from) & (document_of(source, border) == document_of(targets, border))
    scores = jnp.where(valid, targets, N_CTX + targets) + jnp.zeros((N_CTX, N_CTX), jnp.int32)
    order = jnp.argsort(scores, axis=1)
    chosen = order[:, :SLOTS].astype(jnp.int32)
    keep = jnp.take_along_axis(valid + jnp.zeros((N_CTX, N_CTX), bool), chosen, axis=1)
    source_full = source + jnp.zeros((N_CTX, N_CTX), jnp.int32)
    source_list = jnp.where(keep, jnp.take_along_axis(source_full, chosen, axis=1), -1)
    target_list = jnp.where(keep, chosen, -1)
    return jnp.stack([source_list, target_list], axis=-1).astype(jnp.int32)


def loguniform_between(key, lowest, highest):
    spread = jax.random.uniform(key, (D,), jnp.float32)
    return jnp.exp(jnp.log(lowest) + spread * (jnp.log(highest) - jnp.log(lowest)))


def draw_decay_rate(key, part):
    slow_share = 0.5
    band_share = 0.85
    slow_floor = 1.8
    picker = jax.random.uniform(jax.random.fold_in(key, 11), (D,), jnp.float32)
    slow_rates = loguniform_between(jax.random.fold_in(key, 12), slow_floor / SEQ, 2.3 / SEQ)
    band_rates = loguniform_between(jax.random.fold_in(key, 13), 2.7 / SEQ, 6.0 / SEQ)
    fast_rates = loguniform_between(jax.random.fold_in(key, 14), 0.02, 0.033)
    return jnp.where(picker < slow_share, slow_rates, jnp.where(picker < band_share, band_rates, fast_rates)).astype(jnp.float32)


def draw_lag_profile(key, part):
    fraction = jnp.arange(SEQ, dtype=jnp.float32) / SEQ
    values = jnp.clip(jax.random.normal(jax.random.fold_in(key, 21), (SEQ,), jnp.float32), -4.0, 4.0)
    envelope = 1.0 + 0.1 * jnp.exp(6.0 * fraction)
    return (values * envelope / jnp.sqrt(jnp.float32(SEQ))).astype(jnp.float32)


def levels(key, shape, shards, smallest, top_value):
    factor_of, own = 1.0, jax.random.fold_in(key, 6)
    for axis_at, blocks in shards:
        heights = jnp.exp(jax.random.uniform(jax.random.fold_in(own, axis_at), (blocks,), jnp.float32, smallest / len(shards), top_value / len(shards)))
        factor_of = factor_of * jnp.repeat(heights, shape[axis_at] // blocks).reshape([-1 if axis == axis_at else 1 for axis in range(len(shape))])
    return factor_of


def scatter_about(own_key, shape, scale, limit, cuts=(), kind=jnp.bfloat16):
    drawn = jax.random.normal(own_key, shape, jnp.float32) * scale
    if len(cuts) > 0:
        drawn = levels(own_key, shape, cuts, -0.22, 0.18) * drawn
    return jnp.clip(drawn, min=-limit, max=limit).astype(kind)


def setup_inputs(seed: int = 0, part: int = 0) -> dict:
    arg_keys = jax.random.split(jax.random.key(seed), 9)
    part_keys = jax.random.split(jax.random.fold_in(arg_keys[8], part), 9)
    query_rows = scatter_about(part_keys[0], (SEQ, D), 1.0, 6.0, ((0, 16),))
    key_rows = scatter_about(part_keys[1], (SEQ, D), 1.0, 6.0, ((0, 16),))
    value_rows = scatter_about(part_keys[2], (SEQ, D), 1.0, 6.0, ((0, 16),))
    conv_taps = scatter_about(arg_keys[3], (3, 3, D), 3 ** -0.5, 3.5, (), jnp.float32)
    decay_rate = draw_decay_rate(jax.random.fold_in(arg_keys[8], 71), part)
    lag_profile = draw_lag_profile(jax.random.fold_in(arg_keys[8], 71), part)
    skip_gain = jnp.clip(jax.random.uniform(arg_keys[6], (D,), jnp.float32, 0.5, 1.5), 0.5, 1.5)
    pair_lists = draw_pair_lists(jax.random.fold_in(jax.random.fold_in(arg_keys[8], part), 71), part)
    return {"query_rows": query_rows, "key_rows": key_rows, "value_rows": value_rows, "conv_taps": conv_taps, "decay_rate": decay_rate, "lag_profile": lag_profile, "skip_gain": skip_gain, "pair_lists": pair_lists}


def short_conv(rows_in, conv_taps):
    values = rows_in.astype(jnp.float32)
    length = values.shape[0]
    padded = jnp.concatenate([jnp.zeros((2, values.shape[1]), jnp.float32), values], axis=0)
    return conv_taps[0] * padded[2:] + conv_taps[1] * padded[1:length + 1] + conv_taps[2] * padded[:length]


def toeplitz_of(window, span_rows):
    reverse_win = window[::-1]
    extended = jnp.concatenate([reverse_win, jnp.zeros((1,), reverse_win.dtype)])
    tiled = jnp.tile(extended, span_rows + 1)
    start = span_rows - 1
    flat_part = tiled[start:start + span_rows * (2 * span_rows - 1)]
    return flat_part.reshape(span_rows, 2 * span_rows - 1)[:, :span_rows]


def block_term(source, span_gap, decay_rate, padded_lag, span_rows):
    gap_rows = (span_gap * span_rows).astype(jnp.int32)
    window = lax.dynamic_slice_in_dim(padded_lag, gap_rows + 1, 2 * span_rows - 1)
    toeplitz = toeplitz_of(window, span_rows)
    positions = jnp.arange(span_rows, dtype=jnp.float32)
    scaled = source.astype(jnp.float32) * jnp.exp(decay_rate[None, :] * positions[:, None])
    mixed = jnp.dot(toeplitz, scaled, precision=lax.Precision.HIGHEST, preferred_element_type=jnp.float32)
    distance = positions[:, None] + gap_rows.astype(jnp.float32)
    return (mixed * jnp.exp(-decay_rate[None, :] * distance)).astype(jnp.bfloat16)


def reference(query_rows, key_rows, value_rows, conv_taps, decay_rate, lag_profile, skip_gain, pair_lists):
    query_feat = short_conv(query_rows, conv_taps[0])
    key_feat = short_conv(key_rows, conv_taps[1])
    value_feat = short_conv(value_rows, conv_taps[2])
    gated = (key_feat * value_feat).astype(jnp.bfloat16)
    spans = gated.reshape(N_CTX, TOK_DEV, D)
    sources = pair_lists[:, :, 0].reshape(-1)
    targets = pair_lists[:, :, 1].reshape(-1)
    span_ids = jnp.arange(N_CTX, dtype=jnp.int32)
    live = jnp.any((sources[:, None, None] == span_ids[None, :, None]) & (targets[:, None, None] == span_ids[None, None, :]), axis=0)
    padded_lag = jnp.concatenate([jnp.zeros((TOK_DEV,), jnp.float32), lag_profile])

    def per_target(target):
        def add_source(anchor, running):
            def compute_block():
                return block_term(spans[anchor], target - anchor, decay_rate, padded_lag, TOK_DEV).astype(jnp.float32)

            def zero_block():
                return jnp.zeros((TOK_DEV, D), jnp.float32)

            return running + lax.cond(live[anchor, target], compute_block, zero_block)

        return lax.fori_loop(0, N_CTX, add_source, jnp.zeros((TOK_DEV, D), jnp.float32))

    long_conv = lax.map(per_target, span_ids).reshape(SEQ, D)
    return (query_feat * (long_conv + skip_gain[None, :] * gated.astype(jnp.float32))).astype(jnp.bfloat16)
```

```python
import functools

import jax
import jax.numpy as jnp
from jax import lax
from jax.experimental import pallas as pl
from jax.experimental.pallas import tpu as pltpu
from jax.sharding import PartitionSpec as P

MESH = pl.DeviceIdType.MESH


def kernel(
    n, rows, cw,
    q_ref, k_ref, v_ref, taps_ref, decay_ref, lag_ref, skip_ref, keep_ref,
    out_ref,
    rim_out, rim_in, gated, qfeat, spans, scaled, masked, toep, result, landed,
    rim_sem, send1, recv1, send2, recv2,
):
    me = lax.axis_index("ctx")
    wide = 2 * rows
    half = n // 2

    barrier = pltpu.get_barrier_semaphore()

    def greet(k, c):
        p = lax.rem(me + k, n)
        pl.semaphore_signal(barrier, inc=1, device_id={"ctx": p}, device_id_type=MESH)
        return c

    lax.fori_loop(1, n, greet, 0)

    for index, ref in enumerate((q_ref, k_ref, v_ref)):
        tail = ref[rows - 16 :, :].astype(jnp.float32)
        rim_out[2 * index : 2 * index + 2, :] = tail[14:16]
    rim_out[6:8, :] = jnp.zeros((2, rim_out.shape[1]), jnp.float32)

    pl.semaphore_wait(barrier, n - 1)

    def rim_copy(to):
        return pltpu.make_async_remote_copy(
            src_ref=rim_out, dst_ref=rim_in, send_sem=rim_sem.at[0], recv_sem=rim_sem.at[1],
            device_id={"ctx": to}, device_id_type=MESH,
        )

    @pl.when(me < n - 1)
    def _():
        rim_copy(me + 1).start()

    @pl.when(me == 0)
    def _():
        rim_in[...] = jnp.zeros_like(rim_in)

    @pl.when(me > 0)
    def _():
        rim_copy(me - 1).wait_recv()

    row = lax.broadcasted_iota(jnp.int32, (rows, cw), 0)

    def feature(ref, index, cols):
        x = ref[:, cols].astype(jnp.float32)
        one = rim_in[2 * index + 1 : 2 * index + 2, cols]
        two = rim_in[2 * index : 2 * index + 1, cols]
        x1 = jnp.where(row == 0, one, pltpu.roll(x, 1, 0))
        x2 = jnp.where(row == 0, two, jnp.where(row == 1, one, pltpu.roll(x, 2, 0)))
        return (
            taps_ref[index, 0:1, cols] * x
            + taps_ref[index, 1:2, cols] * x1
            + taps_ref[index, 2:3, cols] * x2
        )

    def columns(p):
        return pl.ds(pl.multiple_of(p * cw, cw), cw)

    def forward(p, sender):
        return pltpu.make_async_remote_copy(
            src_ref=gated.at[p], dst_ref=spans.at[sender],
            send_sem=send1.at[p], recv_sem=recv1.at[sender],
            device_id={"ctx": p}, device_id_type=MESH,
        )

    def backward(p, sender):
        return pltpu.make_async_remote_copy(
            src_ref=result.at[p], dst_ref=landed.at[sender],
            send_sem=send2.at[p], recv_sem=recv2.at[sender],
            device_id={"ctx": p}, device_id_type=MESH,
        )

    def gate(k, c):
        p = lax.rem(me + half + k, n)
        cols = columns(p)
        value = (feature(k_ref, 1, cols) * feature(v_ref, 2, cols)).astype(jnp.bfloat16)
        gated[p] = value

        @pl.when(p != me)
        def _():
            forward(p, me).start()

        @pl.when(p == me)
        def _():
            spans[me] = value

        return c

    lax.fori_loop(0, n, gate, 0)

    def build(d, c):
        upper = lag_ref[:, pl.ds(pl.multiple_of(d * wide, wide), wide)]
        below = jnp.maximum(d - 1, 0)
        lower = lag_ref[:, pl.ds(pl.multiple_of(below * wide, wide), wide)]
        lower = jnp.where(d > 0, lower, 0.0)
        window = jnp.broadcast_to(jnp.concatenate([upper, lower], axis=1), (wide, 2 * wide))
        turned = pltpu.roll(window, 0, 1, stride=1, stride_axis=0)[:, :wide]
        toep[d] = turned.T.astype(jnp.bfloat16)
        return c

    lax.fori_loop(0, half, build, 0)

    def query(p, c):
        qfeat[p] = feature(q_ref, 0, columns(p))
        return c

    lax.fori_loop(0, n, query, 0)

    rate = decay_ref[:, columns(me)]
    place = lax.broadcasted_iota(jnp.int32, (wide, cw), 0).astype(jnp.float32)
    grow = jnp.exp(rate * place)
    fade = jnp.exp(-rate * place)
    step_fade = jnp.exp(-rate * wide)

    def keep_of(j):
        return keep_ref[pl.ds(j, 1), 0:1]

    def target(i, c):
        for part in range(2):
            source = 2 * i + part

            @pl.when(source != me)
            def _():
                forward(me, source).wait_recv()

        first = spans[2 * i].astype(jnp.float32) * grow[:rows]
        second = spans[2 * i + 1].astype(jnp.float32) * grow[rows:]
        keep_first = keep_of(2 * i)
        keep_second = keep_of(2 * i + 1)
        scaled[i, 0:rows, :] = first.astype(jnp.bfloat16)
        masked[i, 0:rows, :] = (first * keep_second).astype(jnp.bfloat16)
        masked[i, rows:wide, :] = second.astype(jnp.bfloat16)

        def source_step(j, acc):
            both = keep_of(2 * j) * keep_of(2 * j + 1)
            return acc * (step_fade * both) + jnp.dot(
                toep[i - j], masked[j], preferred_element_type=jnp.float32
            )

        acc = lax.fori_loop(0, i, source_step, jnp.zeros((wide, cw), jnp.float32))
        top = acc[:rows] * (step_fade * keep_first) + jnp.dot(
            toep[0, 0:rows, 0:rows], scaled[i, 0:rows, :], preferred_element_type=jnp.float32
        )
        bottom = acc[rows:] * (step_fade * keep_first * keep_second) + jnp.dot(
            toep[0, rows:wide, :], masked[i], preferred_element_type=jnp.float32
        )
        for part, value in enumerate((top * fade[:rows], bottom * fade[rows:])):
            reader = 2 * i + part
            value = value.astype(jnp.bfloat16)
            result[reader] = value

            @pl.when(reader != me)
            def _():
                backward(reader, me).start()

            @pl.when(reader == me)
            def _():
                landed[me] = value

        return c

    lax.fori_loop(0, half, target, 0)

    def finish(k, c):
        p = lax.rem(me + k, n)

        @pl.when(p != me)
        def _():
            backward(me, p).wait_recv()

        cols = columns(p)
        direct = skip_ref[:, cols] * gated[p].astype(jnp.float32)
        out_ref[:, cols] = (qfeat[p] * (landed[p].astype(jnp.float32) + direct)).astype(
            jnp.bfloat16
        )
        return c

    lax.fori_loop(0, n, finish, 0)

    def drain(k, c):
        p = lax.rem(me + k, n)
        forward(p, me).wait_send()
        backward(p, me).wait_send()
        return c

    lax.fori_loop(1, n, drain, 0)

    @pl.when(me < n - 1)
    def _():
        rim_copy(me + 1).wait_send()


def on_device(
    query_rows, key_rows, value_rows, conv_taps, decay_rate, lag_profile, skip_gain, pair_lists
):
    rows, channels = query_rows.shape
    n = lax.axis_size("ctx")
    cw = channels // n
    half = n // 2
    wide = 2 * rows
    sources, targets = pair_lists[:, :, 0], pair_lists[:, :, 1]
    border = 1 + jnp.max(jnp.where(sources == 0, targets, -1))
    keep = (lax.broadcasted_iota(jnp.int32, (n, 128), 0) != border).astype(jnp.float32)
    vmem = pl.BlockSpec(memory_space=pltpu.VMEM)
    return pl.pallas_call(
        functools.partial(kernel, n, rows, cw),
        out_shape=jax.ShapeDtypeStruct((rows, channels), jnp.bfloat16),
        in_specs=[vmem] * 8,
        out_specs=vmem,
        scratch_shapes=[
            pltpu.VMEM((8, channels), jnp.float32),
            pltpu.VMEM((8, channels), jnp.float32),
            pltpu.VMEM((n, rows, cw), jnp.bfloat16),
            pltpu.VMEM((n, rows, cw), jnp.float32),
            pltpu.VMEM((n, rows, cw), jnp.bfloat16),
            pltpu.VMEM((half, wide, cw), jnp.bfloat16),
            pltpu.VMEM((half, wide, cw), jnp.bfloat16),
            pltpu.VMEM((half, wide, wide), jnp.bfloat16),
            pltpu.VMEM((n, rows, cw), jnp.bfloat16),
            pltpu.VMEM((n, rows, cw), jnp.bfloat16),
            pltpu.SemaphoreType.DMA((2,)),
            pltpu.SemaphoreType.DMA((n,)),
            pltpu.SemaphoreType.DMA((n,)),
            pltpu.SemaphoreType.DMA((n,)),
            pltpu.SemaphoreType.DMA((n,)),
        ],
        compiler_params=pltpu.CompilerParams(
            collective_id=0, has_side_effects=True, vmem_limit_bytes=48 * 1024 * 1024
        ),
    )(
        query_rows, key_rows, value_rows, conv_taps, decay_rate.reshape(1, -1),
        lag_profile.reshape(1, -1), skip_gain.reshape(1, -1), keep,
    )


def solution(mesh):
    rows = P(("group", "ctx"), None)
    return jax.shard_map(
        on_device,
        mesh=mesh,
        in_specs=(rows, rows, rows, P(), P(), P(), P(), P("group", None, None)),
        out_specs=rows,
        check_vma=False,
    )
```

```python
import functools

import jax
import jax.numpy as jnp
from jax import lax
from jax.experimental import pallas as pl
from jax.experimental.pallas import tpu as pltpu
from jax.sharding import PartitionSpec as P

MESH = pl.DeviceIdType.MESH
CHUNK = 256


def kernel(
    n, rows, chunks, width,
    q_hbm, k_hbm, v_hbm, taps_hbm, decay_ref, lag_ref, skip_ref, keep_ref,
    out_ref,
    q_ref, k_ref, v_ref, taps_ref, rim_out, rim_in, gated, qfeat, spans, scaled, masked, toep,
    outbox, inbox, start_acc, result, landed,
    load_sem, rim_sem, send1, recv1, send2, recv2, send_box, recv_box,
):
    me = lax.axis_index("ctx")
    wide = 2 * rows
    members = n // 2
    supers = n // 4
    boxed = n // 8
    part = me // members
    base = part * members
    mine = me - base

    loads = [
        pltpu.make_async_copy(src, dst, load_sem.at[index])
        for index, (src, dst) in enumerate(
            ((k_hbm, k_ref), (v_hbm, v_ref), (taps_hbm, taps_ref), (q_hbm, q_ref))
        )
    ]
    for load in loads:
        load.start()

    barrier = pltpu.get_barrier_semaphore()

    def greet(k, c):
        p = lax.rem(me + k, n)
        pl.semaphore_signal(barrier, inc=1, device_id={"ctx": p}, device_id_type=MESH)
        return c

    lax.fori_loop(1, n, greet, 0)
    for load in loads:
        load.wait()

    for index, ref in enumerate((q_ref, k_ref, v_ref)):
        tail = ref[rows - 16 :, :].astype(jnp.float32)
        rim_out[2 * index : 2 * index + 2, :] = tail[14:16]
    rim_out[6:8, :] = jnp.zeros((2, rim_out.shape[1]), jnp.float32)

    pl.semaphore_wait(barrier, n - 1)

    def rim_copy(to):
        return pltpu.make_async_remote_copy(
            src_ref=rim_out, dst_ref=rim_in, send_sem=rim_sem.at[0], recv_sem=rim_sem.at[1],
            device_id={"ctx": to}, device_id_type=MESH,
        )

    @pl.when(me < n - 1)
    def _():
        rim_copy(me + 1).start()

    @pl.when(me == 0)
    def _():
        rim_in[...] = jnp.zeros_like(rim_in)

    def build(d, c):
        upper = lag_ref[:, pl.ds(pl.multiple_of(d * wide, wide), wide)]
        below = jnp.maximum(d - 1, 0)
        lower = lag_ref[:, pl.ds(pl.multiple_of(below * wide, wide), wide)]
        lower = jnp.where(d > 0, lower, 0.0)
        window = jnp.broadcast_to(jnp.concatenate([upper, lower], axis=1), (wide, 2 * wide))
        turned = pltpu.roll(window, 0, 1, stride=1, stride_axis=0)[:, :wide]
        toep[d] = turned.T.astype(jnp.bfloat16)
        return c

    @pl.when(me > 0)
    def _():
        rim_copy(me - 1).wait_recv()

    row = lax.broadcasted_iota(jnp.int32, (rows, width), 0)

    def feature(ref, index, cols):
        x = ref[:, cols].astype(jnp.float32)
        one = rim_in[2 * index + 1 : 2 * index + 2, cols]
        two = rim_in[2 * index : 2 * index + 1, cols]
        x1 = jnp.where(row == 0, one, pltpu.roll(x, 1, 0))
        x2 = jnp.where(row == 0, two, jnp.where(row == 1, one, pltpu.roll(x, 2, 0)))
        return (
            taps_ref[index, 0:1, cols] * x
            + taps_ref[index, 1:2, cols] * x1
            + taps_ref[index, 2:3, cols] * x2
        )

    def columns(c, p):
        return pl.ds(pl.multiple_of((p * chunks + c) * width, width), width)

    def forward(c, p, sender):
        return pltpu.make_async_remote_copy(
            src_ref=gated.at[c, p], dst_ref=spans.at[c, sender],
            send_sem=send1.at[c, p], recv_sem=recv1.at[c, sender],
            device_id={"ctx": base + p}, device_id_type=MESH,
        )

    def backward(c, p, sender):
        return pltpu.make_async_remote_copy(
            src_ref=result.at[c, p], dst_ref=landed.at[c, sender],
            send_sem=send2.at[c, p], recv_sem=recv2.at[c, sender],
            device_id={"ctx": base + p}, device_id_type=MESH,
        )

    def box_copy(c, to):
        return pltpu.make_async_remote_copy(
            src_ref=outbox.at[c], dst_ref=inbox.at[c],
            send_sem=send_box.at[c], recv_sem=recv_box.at[c],
            device_id={"ctx": to}, device_id_type=MESH,
        )

    for c in range(chunks):

        def gate(k, carry, c=c):
            p = lax.rem(mine + members // 2 + k, members)
            cols = columns(c, p)
            value = (feature(k_ref, 1, cols) * feature(v_ref, 2, cols)).astype(jnp.bfloat16)
            gated[c, p] = value

            @pl.when(p != mine)
            def _():
                forward(c, p, mine).start()

            @pl.when(p == mine)
            def _():
                spans[c, mine] = value

            return carry

        lax.fori_loop(0, members, gate, 0)

    lax.fori_loop(0, n // 2, build, 0)

    place = lax.broadcasted_iota(jnp.int32, (wide, width), 0).astype(jnp.float32)

    def rate_of(c):
        return decay_ref[:, columns(c, mine)]

    def keep_of(j):
        return keep_ref[pl.ds(j, 1), 0:1]

    early = keep_ref[n : n + 1, 0:1] > 0.5

    def matmul(a, b):
        return jnp.dot(a, b, preferred_element_type=jnp.float32)

    def prepare(c):
        grow = jnp.exp(rate_of(c) * place)

        def scale(i, carry):
            for side in range(2):
                source = 2 * i + side

                @pl.when(source != mine)
                def _():
                    forward(c, mine, source).wait_recv()

            first = spans[c, 2 * i].astype(jnp.float32) * grow[:rows]
            second = (spans[c, 2 * i + 1].astype(jnp.float32) * grow[rows:]).astype(jnp.bfloat16)
            scaled[c, i] = first.astype(jnp.bfloat16)
            masked[c, i, 0:rows, :] = (first * keep_of(base + 2 * i + 1)).astype(jnp.bfloat16)
            masked[c, i, rows:wide, :] = second
            return carry

        lax.fori_loop(0, supers, scale, 0)

    def post(c):
        step_fade = jnp.exp(-rate_of(c) * wide)
        for m in range(boxed):
            acc = matmul(toep[supers + m], masked[c, 0])
            for j in range(1, supers):
                acc = acc * step_fade + matmul(toep[supers + m - j], masked[c, j])
            source = masked[c, supers - boxed + m].astype(jnp.float32)
            outbox[c, m] = jnp.where(early, source, acc).astype(jnp.bfloat16)
        box_copy(c, me + members).start()

    def local(c):
        rate = rate_of(c)
        fade = jnp.exp(-rate * place)
        step_fade = jnp.exp(-rate * wide)

        def target(i, carry):
            @pl.when(part == 0)
            def _():
                start_acc[...] = jnp.zeros_like(start_acc)

            @pl.when(part == 1)
            def _():
                acc = matmul(toep[i + boxed], inbox[c, 0])
                for m in range(1, boxed):
                    span = 2 * (supers - boxed + m)
                    both = keep_of(span) * keep_of(span + 1)
                    acc = acc * (step_fade * both) + matmul(toep[i + boxed - m], inbox[c, m])
                partial = inbox[c, jnp.minimum(i, boxed - 1)].astype(jnp.float32)
                partial = jnp.where(i < boxed, partial, 0.0)
                start_acc[...] = jnp.where(early, acc, partial)

            def source_step(j, acc):
                span = base + 2 * j
                both = keep_of(span) * keep_of(span + 1)
                return acc * (step_fade * both) + matmul(toep[i - j], masked[c, j])

            acc = lax.fori_loop(0, i, source_step, start_acc[...])
            keep_first = keep_of(base + 2 * i)
            keep_second = keep_of(base + 2 * i + 1)
            top = acc[:rows] * (step_fade * keep_first) + matmul(
                toep[0, 0:rows, 0:rows], scaled[c, i]
            )
            bottom = acc[rows:] * (step_fade * keep_first * keep_second) + matmul(
                toep[0, rows:wide, :], masked[c, i]
            )
            for side, value in enumerate((top * fade[:rows], bottom * fade[rows:])):
                reader = 2 * i + side
                value = value.astype(jnp.bfloat16)
                result[c, reader] = value

                @pl.when(reader != mine)
                def _():
                    backward(c, reader, mine).start()

                @pl.when(reader == mine)
                def _():
                    landed[c, mine] = value

            return carry

        lax.fori_loop(0, supers, target, 0)

    for c in range(chunks):
        prepare(c)

        @pl.when(part == 0)
        def _():
            post(c)

    def query(p, carry):
        for c in range(chunks):
            qfeat[c, p] = feature(q_ref, 0, columns(c, p))
        return carry

    lax.fori_loop(0, members, query, 0)

    for c in range(chunks):

        @pl.when(part == 1)
        def _():
            box_copy(c, me - members).wait_recv()

        local(c)

    for c in range(chunks):

        def finish(k, carry, c=c):
            p = lax.rem(mine + k, members)

            @pl.when(p != mine)
            def _():
                backward(c, mine, p).wait_recv()

            cols = columns(c, p)
            direct = skip_ref[:, cols] * gated[c, p].astype(jnp.float32)
            out_ref[:, cols] = (
                qfeat[c, p] * (landed[c, p].astype(jnp.float32) + direct)
            ).astype(jnp.bfloat16)
            return carry

        lax.fori_loop(0, members, finish, 0)

    def drain(k, carry):
        p = lax.rem(mine + k, members)
        for c in range(chunks):
            forward(c, p, mine).wait_send()
            backward(c, p, mine).wait_send()
        return carry

    lax.fori_loop(1, members, drain, 0)

    @pl.when(part == 0)
    def _():
        for c in range(chunks):
            box_copy(c, me + members).wait_send()

    @pl.when(me < n - 1)
    def _():
        rim_copy(me + 1).wait_send()


def on_device(
    query_rows, key_rows, value_rows, conv_taps, decay_rate, lag_profile, skip_gain, pair_lists
):
    rows, channels = query_rows.shape
    n = lax.axis_size("ctx")
    members, supers, boxed, wide = n // 2, n // 4, n // 8, 2 * rows
    share = channels // members
    width = min(CHUNK, max(128, share // 2))
    chunks = share // width
    sources, targets = pair_lists[:, :, 0], pair_lists[:, :, 1]
    border = 1 + jnp.max(jnp.where(sources == 0, targets, -1))
    index = lax.broadcasted_iota(jnp.int32, (n + 8, 128), 0)
    keep = jnp.where(index == n, border <= members, index != border).astype(jnp.float32)
    vmem = pl.BlockSpec(memory_space=pltpu.VMEM)
    hbm = pl.BlockSpec(memory_space=pltpu.HBM)
    bf16, f32 = jnp.bfloat16, jnp.float32
    piece = (chunks, members, rows, width)
    dma = pltpu.SemaphoreType.DMA
    return pl.pallas_call(
        functools.partial(kernel, n, rows, chunks, width),
        out_shape=jax.ShapeDtypeStruct((rows, channels), bf16),
        in_specs=[hbm] * 4 + [vmem] * 4,
        out_specs=vmem,
        scratch_shapes=[
            pltpu.VMEM((rows, channels), bf16),
            pltpu.VMEM((rows, channels), bf16),
            pltpu.VMEM((rows, channels), bf16),
            pltpu.VMEM(conv_taps.shape, f32),
            pltpu.VMEM((8, channels), f32),
            pltpu.VMEM((8, channels), f32),
            pltpu.VMEM(piece, bf16),
            pltpu.VMEM(piece, f32),
            pltpu.VMEM(piece, bf16),
            pltpu.VMEM((chunks, supers, rows, width), bf16),
            pltpu.VMEM((chunks, supers, wide, width), bf16),
            pltpu.VMEM((n // 2, wide, wide), bf16),
            pltpu.VMEM((chunks, boxed, wide, width), bf16),
            pltpu.VMEM((chunks, boxed, wide, width), bf16),
            pltpu.VMEM((wide, width), f32),
            pltpu.VMEM(piece, bf16),
            pltpu.VMEM(piece, bf16),
            dma((4,)),
            dma((2,)),
            dma((chunks, members)),
            dma((chunks, members)),
            dma((chunks, members)),
            dma((chunks, members)),
            dma((chunks,)),
            dma((chunks,)),
        ],
        compiler_params=pltpu.CompilerParams(
            collective_id=0, has_side_effects=True, vmem_limit_bytes=48 * 1024 * 1024
        ),
    )(
        query_rows, key_rows, value_rows, conv_taps, decay_rate.reshape(1, -1),
        lag_profile.reshape(1, -1), skip_gain.reshape(1, -1), keep,
    )


def solution(mesh):
    rows = P(("group", "ctx"), None)
    return jax.shard_map(
        on_device,
        mesh=mesh,
        in_specs=(rows, rows, rows, P(), P(), P(), P(), P("group", None, None)),
        out_specs=rows,
        check_vma=False,
    )
```

```python
import functools

import jax
import jax.numpy as jnp
from jax import lax
from jax.experimental import pallas as pl
from jax.experimental.pallas import tpu as pltpu
from jax.sharding import PartitionSpec as P

MESH = pl.DeviceIdType.MESH
CHUNK = 256


def kernel(
    n, rows, chunks, width,
    q_hbm, k_hbm, v_hbm, taps_hbm, decay_hbm, lag_hbm, skip_hbm, pairs_hbm,
    out_ref,
    q_ref, k_ref, v_ref, taps_ref, decay_ref, lag_ref, skip_ref, pairs_ref, rim_out, rim_in, gated, qfeat, spans, scaled, masked, toep,
    outbox, inbox, partial_sum, result, landed,
    load_sem, rim_sem, send1, recv1, send2, recv2, send_box, recv_box,
):
    me = lax.axis_index("ctx")
    wide = 2 * rows
    members = n // 2
    supers = n // 4
    boxed = n // 8
    part = me // members
    base = part * members
    mine = me - base

    loads = [
        pltpu.make_async_copy(src, dst, load_sem.at[index])
        for index, (src, dst) in enumerate(
            (
                (k_hbm, k_ref), (v_hbm, v_ref), (q_hbm, q_ref), (taps_hbm, taps_ref),
                (lag_hbm, lag_ref), (decay_hbm, decay_ref), (skip_hbm, skip_ref),
                (pairs_hbm, pairs_ref),
            )
        )
    ]
    for load in loads:
        load.start()

    barrier = pltpu.get_barrier_semaphore()

    def greet(k, c):
        p = lax.rem(me + k, n)
        pl.semaphore_signal(barrier, inc=1, device_id={"ctx": p}, device_id_type=MESH)
        return c

    lax.fori_loop(1, n, greet, 0)
    for load in loads:
        load.wait()

    for index, ref in enumerate((q_ref, k_ref, v_ref)):
        tail = ref[rows - 16 :, :].astype(jnp.float32)
        rim_out[2 * index : 2 * index + 2, :] = tail[14:16]
    rim_out[6:8, :] = jnp.zeros((2, rim_out.shape[1]), jnp.float32)

    def build(d, c):
        upper = lag_ref[:, pl.ds(pl.multiple_of(d * wide, wide), wide)]
        below = jnp.maximum(d - 1, 0)
        lower = lag_ref[:, pl.ds(pl.multiple_of(below * wide, wide), wide)]
        lower = jnp.where(d > 0, lower, 0.0)
        window = jnp.broadcast_to(jnp.concatenate([upper, lower], axis=1), (wide, 2 * wide))
        turned = pltpu.roll(window, 0, 1, stride=1, stride_axis=0)[:, :wide]
        toep[d] = turned.T.astype(jnp.bfloat16)
        return c

    lax.fori_loop(0, n // 2, build, 0)
    pl.semaphore_wait(barrier, n - 1)

    def rim_copy(to):
        return pltpu.make_async_remote_copy(
            src_ref=rim_out, dst_ref=rim_in, send_sem=rim_sem.at[0], recv_sem=rim_sem.at[1],
            device_id={"ctx": to}, device_id_type=MESH,
        )

    @pl.when(me < n - 1)
    def _():
        rim_copy(me + 1).start()

    @pl.when(me == 0)
    def _():
        rim_in[...] = jnp.zeros_like(rim_in)

    @pl.when(me > 0)
    def _():
        rim_copy(me - 1).wait_recv()

    row = lax.broadcasted_iota(jnp.int32, (rows, width), 0)

    def feature(ref, index, cols):
        x = ref[:, cols].astype(jnp.float32)
        one = rim_in[2 * index + 1 : 2 * index + 2, cols]
        two = rim_in[2 * index : 2 * index + 1, cols]
        x1 = jnp.where(row == 0, one, pltpu.roll(x, 1, 0))
        x2 = jnp.where(row == 0, two, jnp.where(row == 1, one, pltpu.roll(x, 2, 0)))
        return (
            taps_ref[index, 0:1, cols] * x
            + taps_ref[index, 1:2, cols] * x1
            + taps_ref[index, 2:3, cols] * x2
        )

    def columns(c, p):
        return pl.ds(pl.multiple_of((p * chunks + c) * width, width), width)

    def forward(c, p, sender):
        return pltpu.make_async_remote_copy(
            src_ref=gated.at[c, p], dst_ref=spans.at[c, sender],
            send_sem=send1.at[c, p], recv_sem=recv1.at[c, sender],
            device_id={"ctx": base + p}, device_id_type=MESH,
        )

    def backward(c, p, sender):
        return pltpu.make_async_remote_copy(
            src_ref=result.at[c, p], dst_ref=landed.at[c, sender],
            send_sem=send2.at[c, p], recv_sem=recv2.at[c, sender],
            device_id={"ctx": base + p}, device_id_type=MESH,
        )

    def box_copy(c, to):
        return pltpu.make_async_remote_copy(
            src_ref=outbox.at[c], dst_ref=inbox.at[c],
            send_sem=send_box.at[c], recv_sem=recv_box.at[c],
            device_id={"ctx": to}, device_id_type=MESH,
        )

    for c in range(chunks):

        def gate(k, carry, c=c):
            p = lax.rem(mine + members // 2 + k, members)
            cols = columns(c, p)
            value = (feature(k_ref, 1, cols) * feature(v_ref, 2, cols)).astype(jnp.bfloat16)
            gated[c, p] = value

            @pl.when(p != mine)
            def _():
                forward(c, p, mine).start()

            @pl.when(p == mine)
            def _():
                spans[c, mine] = value

            return carry

        lax.fori_loop(0, members, gate, 0)

    place = lax.broadcasted_iota(jnp.int32, (wide, width), 0).astype(jnp.float32)

    def rate_of(c):
        return decay_ref[:, columns(c, mine)]

    listed = jnp.where(pairs_ref[:, 0, :] == 0, pairs_ref[:, 1, :], -1)
    border = 1 + jnp.max(jnp.max(listed, axis=1, keepdims=True), axis=0, keepdims=True)
    early = border <= members

    def keep_of(j):
        return jnp.where(border == j, 0.0, 1.0)

    def matmul(a, b):
        return jnp.dot(a, b, preferred_element_type=jnp.float32)

    def prepare(c):
        grow = jnp.exp(rate_of(c) * place)

        def scale(i, carry):
            for side in range(2):
                source = 2 * i + side

                @pl.when(source != mine)
                def _():
                    forward(c, mine, source).wait_recv()

            first = spans[c, 2 * i].astype(jnp.float32) * grow[:rows]
            second = (spans[c, 2 * i + 1].astype(jnp.float32) * grow[rows:]).astype(jnp.bfloat16)
            scaled[c, i] = first.astype(jnp.bfloat16)
            masked[c, i, 0:rows, :] = (first * keep_of(base + 2 * i + 1)).astype(jnp.bfloat16)
            masked[c, i, rows:wide, :] = second
            return carry

        lax.fori_loop(0, supers, scale, 0)

    def post(c):
        step_fade = jnp.exp(-rate_of(c) * wide)
        for m in range(boxed):
            acc = matmul(toep[supers + m], masked[c, 0])
            for j in range(1, supers):
                acc = acc * step_fade + matmul(toep[supers + m - j], masked[c, j])
            source = masked[c, supers - boxed + m].astype(jnp.float32)
            outbox[c, m] = jnp.where(early, source, acc).astype(jnp.bfloat16)
        box_copy(c, me + members).start()

    def publish(c, i, top, bottom):
        for side, value in enumerate((top, bottom)):
            reader = 2 * i + side
            value = value.astype(jnp.bfloat16)
            result[c, reader] = value

            @pl.when(reader != mine)
            def _():
                backward(c, reader, mine).start()

            @pl.when(reader == mine)
            def _():
                landed[c, mine] = value

    def local(c):
        rate = rate_of(c)
        fade = jnp.exp(-rate * place)
        step_fade = jnp.exp(-rate * wide)

        def target(i, carry):
            def source_step(j, acc):
                span = base + 2 * j
                both = keep_of(span) * keep_of(span + 1)
                return acc * (step_fade * both) + matmul(toep[i - j], masked[c, j])

            acc = lax.fori_loop(0, i, source_step, jnp.zeros((wide, width), jnp.float32))
            keep_first = keep_of(base + 2 * i)
            keep_second = keep_of(base + 2 * i + 1)
            top = acc[:rows] * (step_fade * keep_first) + matmul(
                toep[0, 0:rows, 0:rows], scaled[c, i]
            )
            bottom = acc[rows:] * (step_fade * keep_first * keep_second) + matmul(
                toep[0, rows:wide, :], masked[c, i]
            )
            top, bottom = top * fade[:rows], bottom * fade[rows:]

            @pl.when(part == 0)
            def _():
                publish(c, i, top, bottom)

            @pl.when(part == 1)
            def _():
                partial_sum[c, i, 0:rows, :] = top
                partial_sum[c, i, rows:wide, :] = bottom

            return carry

        lax.fori_loop(0, supers, target, 0)

    def join(c):
        box_copy(c, me - members).wait_recv()
        rate = rate_of(c)
        step_fade = jnp.exp(-rate * wide)
        fade = jnp.exp(-rate * (place + wide))

        def target(i, far_fade):
            acc = matmul(toep[i + boxed], inbox[c, 0])
            for m in range(1, boxed):
                span = 2 * (supers - boxed + m)
                both = keep_of(span) * keep_of(span + 1)
                acc = acc * (step_fade * both) + matmul(toep[i + boxed - m], inbox[c, m])
            sent = inbox[c, jnp.minimum(i, boxed - 1)].astype(jnp.float32)
            sent = jnp.where(i < boxed, sent, 0.0)
            acc = jnp.where(early, acc, sent) * far_fade
            last = base + 2 * i
            live_top = jnp.where((border < base) | (border > last), 1.0, 0.0)
            live_bottom = jnp.where((border < base) | (border > last + 1), 1.0, 0.0)
            publish(
                c, i,
                partial_sum[c, i, 0:rows, :] + acc[:rows] * live_top,
                partial_sum[c, i, rows:wide, :] + acc[rows:] * live_bottom,
            )
            return far_fade * step_fade

        lax.fori_loop(0, supers, target, fade)

    for c in range(chunks):
        prepare(c)

        @pl.when(part == 0)
        def _():
            post(c)

    for c in range(chunks):
        local(c)

    def query(p, carry):
        for c in range(chunks):
            qfeat[c, p] = feature(q_ref, 0, columns(c, p))
        return carry

    lax.fori_loop(0, members, query, 0)

    for c in range(chunks):

        @pl.when(part == 1)
        def _():
            join(c)

    for c in range(chunks):

        def finish(k, carry, c=c):
            p = lax.rem(mine + k, members)

            @pl.when(p != mine)
            def _():
                backward(c, mine, p).wait_recv()

            cols = columns(c, p)
            direct = skip_ref[:, cols] * gated[c, p].astype(jnp.float32)
            out_ref[:, cols] = (
                qfeat[c, p] * (landed[c, p].astype(jnp.float32) + direct)
            ).astype(jnp.bfloat16)
            return carry

        lax.fori_loop(0, members, finish, 0)

    def drain(k, carry):
        p = lax.rem(mine + k, members)
        for c in range(chunks):
            forward(c, p, mine).wait_send()
            backward(c, p, mine).wait_send()
        return carry

    lax.fori_loop(1, members, drain, 0)

    @pl.when(part == 0)
    def _():
        for c in range(chunks):
            box_copy(c, me + members).wait_send()

    @pl.when(me < n - 1)
    def _():
        rim_copy(me + 1).wait_send()


def on_device(
    query_rows, key_rows, value_rows, conv_taps, decay_rate, lag_profile, skip_gain, pair_lists
):
    rows, channels = query_rows.shape
    n = lax.axis_size("ctx")
    members, supers, boxed, wide = n // 2, n // 4, n // 8, 2 * rows
    share = channels // members
    width = min(CHUNK, max(128, share // 2))
    chunks = share // width
    pairs = pair_lists.transpose(1, 2, 0)
    vmem = pl.BlockSpec(memory_space=pltpu.VMEM)
    hbm = pl.BlockSpec(memory_space=pltpu.HBM)
    bf16, f32 = jnp.bfloat16, jnp.float32
    piece = (chunks, members, rows, width)
    dma = pltpu.SemaphoreType.DMA
    return pl.pallas_call(
        functools.partial(kernel, n, rows, chunks, width),
        out_shape=jax.ShapeDtypeStruct((rows, channels), bf16),
        in_specs=[hbm] * 8,
        out_specs=vmem,
        scratch_shapes=[
            pltpu.VMEM((rows, channels), bf16),
            pltpu.VMEM((rows, channels), bf16),
            pltpu.VMEM((rows, channels), bf16),
            pltpu.VMEM(conv_taps.shape, f32),
            pltpu.VMEM((1, channels), f32),
            pltpu.VMEM((1, lag_profile.shape[0]), f32),
            pltpu.VMEM((1, channels), f32),
            pltpu.VMEM(pairs.shape, jnp.int32),
            pltpu.VMEM((8, channels), f32),
            pltpu.VMEM((8, channels), f32),
            pltpu.VMEM(piece, bf16),
            pltpu.VMEM(piece, f32),
            pltpu.VMEM(piece, bf16),
            pltpu.VMEM((chunks, supers, rows, width), bf16),
            pltpu.VMEM((chunks, supers, wide, width), bf16),
            pltpu.VMEM((n // 2, wide, wide), bf16),
            pltpu.VMEM((chunks, boxed, wide, width), bf16),
            pltpu.VMEM((chunks, boxed, wide, width), bf16),
            pltpu.VMEM((chunks, supers, wide, width), f32),
            pltpu.VMEM(piece, bf16),
            pltpu.VMEM(piece, bf16),
            dma((8,)),
            dma((2,)),
            dma((chunks, members)),
            dma((chunks, members)),
            dma((chunks, members)),
            dma((chunks, members)),
            dma((chunks,)),
            dma((chunks,)),
        ],
        compiler_params=pltpu.CompilerParams(
            collective_id=0, has_side_effects=True, vmem_limit_bytes=62 * 1024 * 1024
        ),
    )(
        query_rows, key_rows, value_rows, conv_taps, decay_rate.reshape(1, -1),
        lag_profile.reshape(1, -1), skip_gain.reshape(1, -1), pairs,
    )


def solution(mesh):
    rows = P(("group", "ctx"), None)
    return jax.shard_map(
        on_device,
        mesh=mesh,
        in_specs=(rows, rows, rows, P(), P(), P(), P(), P("group", None, None)),
        out_specs=rows,
        check_vma=False,
    )
```

```python
import functools

import jax
import jax.numpy as jnp
from jax import lax
from jax.experimental import pallas as pl
from jax.experimental.pallas import tpu as pltpu
from jax.sharding import PartitionSpec as P

MESH = pl.DeviceIdType.MESH
CHUNK = 128


def kernel(
    n, rows, chunks, width,
    q_hbm, k_hbm, v_hbm, taps_hbm, decay_hbm, lag_hbm, skip_hbm, pairs_hbm,
    out_ref,
    q_ref, k_ref, v_ref, taps_ref, decay_ref, lag_ref, skip_ref, pairs_ref, rim_out, rim_in, gated, qfeat, spans, scaled, masked, toep,
    outbox, inbox, partial_sum, result, landed,
    load_sem, rim_sem, send1, recv1, send2, recv2, send_box, recv_box,
):
    me = lax.axis_index("ctx")
    wide = 2 * rows
    members = n // 2
    supers = n // 4
    boxed = n // 8
    part = me // members
    base = part * members
    mine = me - base

    loads = [
        pltpu.make_async_copy(src, dst, load_sem.at[index])
        for index, (src, dst) in enumerate(
            (
                (k_hbm, k_ref), (v_hbm, v_ref), (q_hbm, q_ref), (taps_hbm, taps_ref),
                (lag_hbm, lag_ref), (decay_hbm, decay_ref), (skip_hbm, skip_ref),
                (pairs_hbm, pairs_ref),
            )
        )
    ]
    for load in loads:
        load.start()

    barrier = pltpu.get_barrier_semaphore()

    def greet(k, c):
        p = lax.rem(me + k, n)
        pl.semaphore_signal(barrier, inc=1, device_id={"ctx": p}, device_id_type=MESH)
        return c

    lax.fori_loop(1, n, greet, 0)
    for load in loads:
        load.wait()

    for index, ref in enumerate((q_ref, k_ref, v_ref)):
        tail = ref[rows - 16 :, :].astype(jnp.float32)
        rim_out[2 * index : 2 * index + 2, :] = tail[14:16]
    rim_out[6:8, :] = jnp.zeros((2, rim_out.shape[1]), jnp.float32)

    def build(d, c):
        upper = lag_ref[:, pl.ds(pl.multiple_of(d * wide, wide), wide)]
        below = jnp.maximum(d - 1, 0)
        lower = lag_ref[:, pl.ds(pl.multiple_of(below * wide, wide), wide)]
        lower = jnp.where(d > 0, lower, 0.0)
        window = jnp.broadcast_to(jnp.concatenate([upper, lower], axis=1), (wide, 2 * wide))
        turned = pltpu.roll(window, 0, 1, stride=1, stride_axis=0)[:, :wide]
        toep[d] = turned.T.astype(jnp.bfloat16)
        return c

    lax.fori_loop(0, n // 2, build, 0)
    pl.semaphore_wait(barrier, n - 1)

    def rim_copy(to):
        return pltpu.make_async_remote_copy(
            src_ref=rim_out, dst_ref=rim_in, send_sem=rim_sem.at[0], recv_sem=rim_sem.at[1],
            device_id={"ctx": to}, device_id_type=MESH,
        )

    @pl.when(me < n - 1)
    def _():
        rim_copy(me + 1).start()

    @pl.when(me == 0)
    def _():
        rim_in[...] = jnp.zeros_like(rim_in)

    @pl.when(me > 0)
    def _():
        rim_copy(me - 1).wait_recv()

    row = lax.broadcasted_iota(jnp.int32, (rows, width), 0)

    def feature(ref, index, cols):
        x = ref[:, cols].astype(jnp.float32)
        one = rim_in[2 * index + 1 : 2 * index + 2, cols]
        two = rim_in[2 * index : 2 * index + 1, cols]
        x1 = jnp.where(row == 0, one, pltpu.roll(x, 1, 0))
        x2 = jnp.where(row == 0, two, jnp.where(row == 1, one, pltpu.roll(x, 2, 0)))
        return (
            taps_ref[index, 0:1, cols] * x
            + taps_ref[index, 1:2, cols] * x1
            + taps_ref[index, 2:3, cols] * x2
        )

    def columns(c, p):
        return pl.ds(pl.multiple_of((p * chunks + c) * width, width), width)

    def forward(c, p, sender):
        return pltpu.make_async_remote_copy(
            src_ref=gated.at[c, p], dst_ref=spans.at[c, sender],
            send_sem=send1.at[c, p], recv_sem=recv1.at[c, sender],
            device_id={"ctx": base + p}, device_id_type=MESH,
        )

    def backward(c, p, sender):
        return pltpu.make_async_remote_copy(
            src_ref=result.at[c, p], dst_ref=landed.at[c, sender],
            send_sem=send2.at[c, p], recv_sem=recv2.at[c, sender],
            device_id={"ctx": base + p}, device_id_type=MESH,
        )

    def box_copy(c, to):
        return pltpu.make_async_remote_copy(
            src_ref=outbox.at[c], dst_ref=inbox.at[c],
            send_sem=send_box.at[c], recv_sem=recv_box.at[c],
            device_id={"ctx": to}, device_id_type=MESH,
        )

    def gate_chunk(c):
        def gate(k, carry):
            p = lax.rem(mine + 1 + k, members)
            cols = columns(c, p)
            value = (feature(k_ref, 1, cols) * feature(v_ref, 2, cols)).astype(jnp.bfloat16)
            gated[c, p] = value

            @pl.when(p != mine)
            def _():
                if c > 0:
                    forward(c - 1, p, mine).wait_send()
                forward(c, p, mine).start()

            @pl.when(p == mine)
            def _():
                spans[c, mine] = value

            return carry

        lax.fori_loop(0, members, gate, 0)

    place = lax.broadcasted_iota(jnp.int32, (wide, width), 0).astype(jnp.float32)

    def rate_of(c):
        return decay_ref[:, columns(c, mine)]

    listed = jnp.where(pairs_ref[:, 0, :] == 0, pairs_ref[:, 1, :], -1)
    border = 1 + jnp.max(jnp.max(listed, axis=1, keepdims=True), axis=0, keepdims=True)
    early = border <= members

    def keep_of(j):
        return jnp.where(border == j, 0.0, 1.0)

    def matmul(a, b):
        return jnp.dot(a, b, preferred_element_type=jnp.float32)

    def prepare(c):
        grow = jnp.exp(rate_of(c) * place)

        def scale(i, carry):
            for side in range(2):
                source = 2 * i + side

                @pl.when(source != mine)
                def _():
                    forward(c, mine, source).wait_recv()

            first = spans[c, 2 * i].astype(jnp.float32) * grow[:rows]
            second = (spans[c, 2 * i + 1].astype(jnp.float32) * grow[rows:]).astype(jnp.bfloat16)
            scaled[c, i] = first.astype(jnp.bfloat16)
            masked[c, i, 0:rows, :] = (first * keep_of(base + 2 * i + 1)).astype(jnp.bfloat16)
            masked[c, i, rows:wide, :] = second
            return carry

        lax.fori_loop(0, supers, scale, 0)

    def post(c):
        step_fade = jnp.exp(-rate_of(c) * wide)
        for m in range(boxed):
            acc = matmul(toep[supers + m], masked[c, 0])
            for j in range(1, supers):
                acc = acc * step_fade + matmul(toep[supers + m - j], masked[c, j])
            source = masked[c, supers - boxed + m].astype(jnp.float32)
            outbox[c, m] = jnp.where(early, source, acc).astype(jnp.bfloat16)
        box_copy(c, me + members).start()

    def publish(c, i, top, bottom):
        for side, value in enumerate((top, bottom)):
            reader = 2 * i + side
            value = value.astype(jnp.bfloat16)
            result[c, reader] = value

            @pl.when(reader != mine)
            def _():
                backward(c, reader, mine).start()

            @pl.when(reader == mine)
            def _():
                landed[c, mine] = value

    def local(c):
        rate = rate_of(c)
        fade = jnp.exp(-rate * place)
        step_fade = jnp.exp(-rate * wide)

        def target(i, carry):
            def source_step(j, acc):
                span = base + 2 * j
                both = keep_of(span) * keep_of(span + 1)
                return acc * (step_fade * both) + matmul(toep[i - j], masked[c, j])

            acc = lax.fori_loop(0, i, source_step, jnp.zeros((wide, width), jnp.float32))
            keep_first = keep_of(base + 2 * i)
            keep_second = keep_of(base + 2 * i + 1)
            top = acc[:rows] * (step_fade * keep_first) + matmul(
                toep[0, 0:rows, 0:rows], scaled[c, i]
            )
            bottom = acc[rows:] * (step_fade * keep_first * keep_second) + matmul(
                toep[0, rows:wide, :], masked[c, i]
            )
            top, bottom = top * fade[:rows], bottom * fade[rows:]

            @pl.when(part == 0)
            def _():
                publish(c, i, top, bottom)

            @pl.when(part == 1)
            def _():
                partial_sum[c, i, 0:rows, :] = top
                partial_sum[c, i, rows:wide, :] = bottom

            return carry

        lax.fori_loop(0, supers, target, 0)

    def join(c):
        box_copy(c, me - members).wait_recv()
        rate = rate_of(c)
        step_fade = jnp.exp(-rate * wide)
        fade = jnp.exp(-rate * (place + wide))

        def target(i, far_fade):
            acc = matmul(toep[i + boxed], inbox[c, 0])
            for m in range(1, boxed):
                span = 2 * (supers - boxed + m)
                both = keep_of(span) * keep_of(span + 1)
                acc = acc * (step_fade * both) + matmul(toep[i + boxed - m], inbox[c, m])
            sent = inbox[c, jnp.minimum(i, boxed - 1)].astype(jnp.float32)
            sent = jnp.where(i < boxed, sent, 0.0)
            acc = jnp.where(early, acc, sent) * far_fade
            last = base + 2 * i
            live_top = jnp.where((border < base) | (border > last), 1.0, 0.0)
            live_bottom = jnp.where((border < base) | (border > last + 1), 1.0, 0.0)
            publish(
                c, i,
                partial_sum[c, i, 0:rows, :] + acc[:rows] * live_top,
                partial_sum[c, i, rows:wide, :] + acc[rows:] * live_bottom,
            )
            return far_fade * step_fade

        lax.fori_loop(0, supers, target, fade)

    gate_chunk(0)
    for c in range(chunks):
        if c + 1 < chunks:
            gate_chunk(c + 1)
        prepare(c)

        @pl.when(part == 0)
        def _():
            post(c)

    for c in range(chunks):

        local(c)

    def query(p, carry):
        for c in range(chunks):
            qfeat[c, p] = feature(q_ref, 0, columns(c, p))
        return carry

    lax.fori_loop(0, members, query, 0)

    for c in range(chunks):

        @pl.when(part == 1)
        def _():
            join(c)

    for c in range(chunks):

        def finish(k, carry, c=c):
            p = lax.rem(mine + k, members)

            @pl.when(p != mine)
            def _():
                backward(c, mine, p).wait_recv()

            cols = columns(c, p)
            direct = skip_ref[:, cols] * gated[c, p].astype(jnp.float32)
            out_ref[:, cols] = (
                qfeat[c, p] * (landed[c, p].astype(jnp.float32) + direct)
            ).astype(jnp.bfloat16)
            return carry

        lax.fori_loop(0, members, finish, 0)

    def drain(k, carry):
        p = lax.rem(mine + k, members)
        forward(chunks - 1, p, mine).wait_send()
        for c in range(chunks):
            backward(c, p, mine).wait_send()
        return carry

    lax.fori_loop(1, members, drain, 0)

    @pl.when(part == 0)
    def _():
        for c in range(chunks):
            box_copy(c, me + members).wait_send()

    @pl.when(me < n - 1)
    def _():
        rim_copy(me + 1).wait_send()


def on_device(
    query_rows, key_rows, value_rows, conv_taps, decay_rate, lag_profile, skip_gain, pair_lists
):
    rows, channels = query_rows.shape
    n = lax.axis_size("ctx")
    members, supers, boxed, wide = n // 2, n // 4, n // 8, 2 * rows
    share = channels // members
    width = min(CHUNK, max(128, share // 2))
    chunks = share // width
    pairs = pair_lists.transpose(1, 2, 0)
    vmem = pl.BlockSpec(memory_space=pltpu.VMEM)
    hbm = pl.BlockSpec(memory_space=pltpu.HBM)
    bf16, f32 = jnp.bfloat16, jnp.float32
    piece = (chunks, members, rows, width)
    dma = pltpu.SemaphoreType.DMA
    return pl.pallas_call(
        functools.partial(kernel, n, rows, chunks, width),
        out_shape=jax.ShapeDtypeStruct((rows, channels), bf16),
        in_specs=[hbm] * 8,
        out_specs=vmem,
        scratch_shapes=[
            pltpu.VMEM((rows, channels), bf16),
            pltpu.VMEM((rows, channels), bf16),
            pltpu.VMEM((rows, channels), bf16),
            pltpu.VMEM(conv_taps.shape, f32),
            pltpu.VMEM((1, channels), f32),
            pltpu.VMEM((1, lag_profile.shape[0]), f32),
            pltpu.VMEM((1, channels), f32),
            pltpu.VMEM(pairs.shape, jnp.int32),
            pltpu.VMEM((8, channels), f32),
            pltpu.VMEM((8, channels), f32),
            pltpu.VMEM(piece, bf16),
            pltpu.VMEM(piece, f32),
            pltpu.VMEM(piece, bf16),
            pltpu.VMEM((chunks, supers, rows, width), bf16),
            pltpu.VMEM((chunks, supers, wide, width), bf16),
            pltpu.VMEM((n // 2, wide, wide), bf16),
            pltpu.VMEM((chunks, boxed, wide, width), bf16),
            pltpu.VMEM((chunks, boxed, wide, width), bf16),
            pltpu.VMEM((chunks, supers, wide, width), f32),
            pltpu.VMEM(piece, bf16),
            pltpu.VMEM(piece, bf16),
            dma((8,)),
            dma((2,)),
            dma((chunks, members)),
            dma((chunks, members)),
            dma((chunks, members)),
            dma((chunks, members)),
            dma((chunks,)),
            dma((chunks,)),
        ],
        compiler_params=pltpu.CompilerParams(
            collective_id=0, has_side_effects=True, vmem_limit_bytes=62 * 1024 * 1024
        ),
    )(
        query_rows, key_rows, value_rows, conv_taps, decay_rate.reshape(1, -1),
        lag_profile.reshape(1, -1), skip_gain.reshape(1, -1), pairs,
    )


def solution(mesh):
    rows = P(("group", "ctx"), None)
    return jax.shard_map(
        on_device,
        mesh=mesh,
        in_specs=(rows, rows, rows, P(), P(), P(), P(), P("group", None, None)),
        out_specs=rows,
        check_vma=False,
    )
```

```python
import functools

import jax
import jax.numpy as jnp
from jax import lax
from jax.experimental import pallas as pl
from jax.experimental.pallas import tpu as pltpu
from jax.sharding import PartitionSpec as P

MESH = pl.DeviceIdType.MESH
CHUNK = 128
STRIPS = 8


def kernel(
    n, rows, chunks, width,
    q_hbm, k_hbm, v_hbm, taps_hbm, decay_hbm, lag_hbm, skip_hbm, pairs_hbm,
    out_hbm,
    out_ref, q_ref, k_ref, v_ref, taps_ref, decay_ref, lag_ref, skip_ref, pairs_ref, rim_out, rim_in, gated, qfeat, spans, scaled, masked, toep,
    outbox, inbox, partial_sum, result, landed,
    load_sem, store_sem, rim_sem, send1, recv1, send2, recv2, send_box, recv_box,
):
    me = lax.axis_index("ctx")
    wide = 2 * rows
    members = n // 2
    supers = n // 4
    boxed = n // 8
    part = me // members
    base = part * members
    mine = me - base

    loads = [
        pltpu.make_async_copy(src, dst, load_sem.at[index])
        for index, (src, dst) in enumerate(
            (
                (k_hbm, k_ref), (v_hbm, v_ref), (q_hbm, q_ref), (taps_hbm, taps_ref),
                (lag_hbm, lag_ref), (decay_hbm, decay_ref), (skip_hbm, skip_ref),
                (pairs_hbm, pairs_ref),
            )
        )
    ]
    for load in loads:
        load.start()

    barrier = pltpu.get_barrier_semaphore()

    def greet(k, c):
        p = lax.rem(me + k, n)
        pl.semaphore_signal(barrier, inc=1, device_id={"ctx": p}, device_id_type=MESH)
        return c

    lax.fori_loop(1, n, greet, 0)
    for load in loads:
        load.wait()

    for index, ref in enumerate((q_ref, k_ref, v_ref)):
        tail = ref[rows - 16 :, :].astype(jnp.float32)
        rim_out[2 * index : 2 * index + 2, :] = tail[14:16]
    rim_out[6:8, :] = jnp.zeros((2, rim_out.shape[1]), jnp.float32)

    def build(d, c):
        upper = lag_ref[:, pl.ds(pl.multiple_of(d * wide, wide), wide)]
        below = jnp.maximum(d - 1, 0)
        lower = lag_ref[:, pl.ds(pl.multiple_of(below * wide, wide), wide)]
        lower = jnp.where(d > 0, lower, 0.0)
        window = jnp.broadcast_to(jnp.concatenate([upper, lower], axis=1), (wide, 2 * wide))
        turned = pltpu.roll(window, 0, 1, stride=1, stride_axis=0)[:, :wide]
        toep[d] = turned.T.astype(jnp.bfloat16)
        return c

    lax.fori_loop(0, n // 2, build, 0)
    pl.semaphore_wait(barrier, n - 1)

    def rim_copy(to):
        return pltpu.make_async_remote_copy(
            src_ref=rim_out, dst_ref=rim_in, send_sem=rim_sem.at[0], recv_sem=rim_sem.at[1],
            device_id={"ctx": to}, device_id_type=MESH,
        )

    @pl.when(me < n - 1)
    def _():
        rim_copy(me + 1).start()

    @pl.when(me == 0)
    def _():
        rim_in[...] = jnp.zeros_like(rim_in)

    @pl.when(me > 0)
    def _():
        rim_copy(me - 1).wait_recv()

    row = lax.broadcasted_iota(jnp.int32, (rows, width), 0)

    def feature(ref, index, cols):
        x = ref[:, cols].astype(jnp.float32)
        one = rim_in[2 * index + 1 : 2 * index + 2, cols]
        two = rim_in[2 * index : 2 * index + 1, cols]
        x1 = jnp.where(row == 0, one, pltpu.roll(x, 1, 0))
        x2 = jnp.where(row == 0, two, jnp.where(row == 1, one, pltpu.roll(x, 2, 0)))
        return (
            taps_ref[index, 0:1, cols] * x
            + taps_ref[index, 1:2, cols] * x1
            + taps_ref[index, 2:3, cols] * x2
        )

    def columns(c, p):
        return pl.ds(pl.multiple_of((p * chunks + c) * width, width), width)

    def forward(c, p, sender):
        return pltpu.make_async_remote_copy(
            src_ref=gated.at[c, p], dst_ref=spans.at[c, sender],
            send_sem=send1.at[c, p], recv_sem=recv1.at[c, sender],
            device_id={"ctx": base + p}, device_id_type=MESH,
        )

    def backward(c, p, sender):
        return pltpu.make_async_remote_copy(
            src_ref=result.at[c, p], dst_ref=landed.at[c, sender],
            send_sem=send2.at[c, p], recv_sem=recv2.at[c, sender],
            device_id={"ctx": base + p}, device_id_type=MESH,
        )

    def box_copy(c, to):
        return pltpu.make_async_remote_copy(
            src_ref=outbox.at[c], dst_ref=inbox.at[c],
            send_sem=send_box.at[c], recv_sem=recv_box.at[c],
            device_id={"ctx": to}, device_id_type=MESH,
        )

    def gate_chunk(c):
        def gate(k, carry):
            p = lax.rem(mine + 1 + k, members)
            cols = columns(c, p)
            value = (feature(k_ref, 1, cols) * feature(v_ref, 2, cols)).astype(jnp.bfloat16)
            gated[c, p] = value

            @pl.when(p != mine)
            def _():
                if c > 0:
                    forward(c - 1, p, mine).wait_send()
                forward(c, p, mine).start()

            @pl.when(p == mine)
            def _():
                spans[c, mine] = value

            return carry

        lax.fori_loop(0, members, gate, 0)

    place = lax.broadcasted_iota(jnp.int32, (wide, width), 0).astype(jnp.float32)

    def rate_of(c):
        return decay_ref[:, columns(c, mine)]

    listed = jnp.where(pairs_ref[:, 0, :] == 0, pairs_ref[:, 1, :], -1)
    border = 1 + jnp.max(jnp.max(listed, axis=1, keepdims=True), axis=0, keepdims=True)
    early = border <= members

    def keep_of(j):
        return jnp.where(border == j, 0.0, 1.0)

    def matmul(a, b):
        return jnp.dot(a, b, preferred_element_type=jnp.float32)

    def prepare(c):
        grow = jnp.exp(rate_of(c) * place)

        def scale(i, carry):
            for side in range(2):
                source = 2 * i + side

                @pl.when(source != mine)
                def _():
                    forward(c, mine, source).wait_recv()

            first = spans[c, 2 * i].astype(jnp.float32) * grow[:rows]
            second = (spans[c, 2 * i + 1].astype(jnp.float32) * grow[rows:]).astype(jnp.bfloat16)
            scaled[c, i] = first.astype(jnp.bfloat16)
            masked[c, i, 0:rows, :] = (first * keep_of(base + 2 * i + 1)).astype(jnp.bfloat16)
            masked[c, i, rows:wide, :] = second
            return carry

        lax.fori_loop(0, supers, scale, 0)

    def post(c):
        step_fade = jnp.exp(-rate_of(c) * wide)
        for m in range(boxed):
            acc = matmul(toep[supers + m], masked[c, 0])
            for j in range(1, supers):
                acc = acc * step_fade + matmul(toep[supers + m - j], masked[c, j])
            source = masked[c, supers - boxed + m].astype(jnp.float32)
            outbox[c, m] = jnp.where(early, source, acc).astype(jnp.bfloat16)
        box_copy(c, me + members).start()

    def publish(c, i, top, bottom):
        for side, value in enumerate((top, bottom)):
            reader = 2 * i + side
            value = value.astype(jnp.bfloat16)
            result[c, reader] = value

            @pl.when(reader != mine)
            def _():
                backward(c, reader, mine).start()

            @pl.when(reader == mine)
            def _():
                landed[c, mine] = value

    def local(c):
        rate = rate_of(c)
        fade = jnp.exp(-rate * place)
        step_fade = jnp.exp(-rate * wide)

        def target(i, carry):
            def source_step(j, acc):
                span = base + 2 * j
                both = keep_of(span) * keep_of(span + 1)
                return acc * (step_fade * both) + matmul(toep[i - j], masked[c, j])

            acc = lax.fori_loop(0, i, source_step, jnp.zeros((wide, width), jnp.float32))
            keep_first = keep_of(base + 2 * i)
            keep_second = keep_of(base + 2 * i + 1)
            top = acc[:rows] * (step_fade * keep_first) + matmul(
                toep[0, 0:rows, 0:rows], scaled[c, i]
            )
            bottom = acc[rows:] * (step_fade * keep_first * keep_second) + matmul(
                toep[0, rows:wide, :], masked[c, i]
            )
            top, bottom = top * fade[:rows], bottom * fade[rows:]

            @pl.when(part == 0)
            def _():
                publish(c, i, top, bottom)

            @pl.when(part == 1)
            def _():
                partial_sum[c, i, 0:rows, :] = top
                partial_sum[c, i, rows:wide, :] = bottom

            return carry

        lax.fori_loop(0, supers, target, 0)

    def join(c):
        box_copy(c, me - members).wait_recv()
        rate = rate_of(c)
        step_fade = jnp.exp(-rate * wide)
        fade = jnp.exp(-rate * (place + wide))

        def target(i, far_fade):
            acc = matmul(toep[i + boxed], inbox[c, 0])
            for m in range(1, boxed):
                span = 2 * (supers - boxed + m)
                both = keep_of(span) * keep_of(span + 1)
                acc = acc * (step_fade * both) + matmul(toep[i + boxed - m], inbox[c, m])
            sent = inbox[c, jnp.minimum(i, boxed - 1)].astype(jnp.float32)
            sent = jnp.where(i < boxed, sent, 0.0)
            acc = jnp.where(early, acc, sent) * far_fade
            last = base + 2 * i
            live_top = jnp.where((border < base) | (border > last), 1.0, 0.0)
            live_bottom = jnp.where((border < base) | (border > last + 1), 1.0, 0.0)
            publish(
                c, i,
                partial_sum[c, i, 0:rows, :] + acc[:rows] * live_top,
                partial_sum[c, i, rows:wide, :] + acc[rows:] * live_bottom,
            )
            return far_fade * step_fade

        lax.fori_loop(0, supers, target, fade)

    gate_chunk(0)
    for c in range(chunks):
        if c + 1 < chunks:
            gate_chunk(c + 1)
        prepare(c)

        @pl.when(part == 0)
        def _():
            post(c)

    for c in range(chunks):

        local(c)

    def query(p, carry):
        for c in range(chunks):
            qfeat[c, p] = feature(q_ref, 0, columns(c, p))
        return carry

    lax.fori_loop(0, members, query, 0)

    for c in range(chunks):

        @pl.when(part == 1)
        def _():
            join(c)

    def store(c, p):
        cols = columns(c, p)
        return pltpu.make_async_copy(out_ref.at[:, cols], out_hbm.at[:, cols], store_sem.at[c, p])

    for c in range(chunks):

        def finish(k, carry, c=c):
            p = lax.rem(mine + k, members)

            @pl.when(p != mine)
            def _():
                backward(c, mine, p).wait_recv()

            cols = columns(c, p)
            direct = skip_ref[:, cols] * gated[c, p].astype(jnp.float32)
            out_ref[:, cols] = (
                qfeat[c, p] * (landed[c, p].astype(jnp.float32) + direct)
            ).astype(jnp.bfloat16)
            store(c, p).start()
            return carry

        lax.fori_loop(0, members, finish, 0)

    def drain(k, carry):
        p = lax.rem(mine + k, members)
        forward(chunks - 1, p, mine).wait_send()
        for c in range(chunks):
            backward(c, p, mine).wait_send()
        return carry

    lax.fori_loop(1, members, drain, 0)

    def stored(p, carry):
        for c in range(chunks):
            store(c, p).wait()
        return carry

    lax.fori_loop(0, members, stored, 0)

    @pl.when(part == 0)
    def _():
        for c in range(chunks):
            box_copy(c, me + members).wait_send()

    @pl.when(me < n - 1)
    def _():
        rim_copy(me + 1).wait_send()


def hand_over(strip, src_ref, dst_ref, held, in_sem, out_sem):
    def load(i):
        part = pl.ds(i * strip, strip)
        return pltpu.make_async_copy(src_ref.at[part], held.at[part], in_sem.at[i])

    def store(i):
        part = pl.ds(i * strip, strip)
        return pltpu.make_async_copy(held.at[part], dst_ref.at[part], out_sem.at[i])

    for i in range(STRIPS):
        load(i).start()
    for i in range(STRIPS):
        load(i).wait()
        store(i).start()
    for i in range(STRIPS):
        store(i).wait()


def on_device(
    query_rows, key_rows, value_rows, conv_taps, decay_rate, lag_profile, skip_gain, pair_lists
):
    rows, channels = query_rows.shape
    n = lax.axis_size("ctx")
    members, supers, boxed, wide = n // 2, n // 4, n // 8, 2 * rows
    share = channels // members
    width = min(CHUNK, max(128, share // 2))
    chunks = share // width
    pairs = pair_lists.transpose(1, 2, 0)
    hbm = pl.BlockSpec(memory_space=pltpu.HBM)
    bf16, f32 = jnp.bfloat16, jnp.float32
    piece = (chunks, members, rows, width)
    dma = pltpu.SemaphoreType.DMA
    held = pl.pallas_call(
        functools.partial(kernel, n, rows, chunks, width),
        out_shape=jax.ShapeDtypeStruct((rows, channels), bf16),
        in_specs=[hbm] * 8,
        out_specs=hbm,
        scratch_shapes=[
            pltpu.VMEM((rows, channels), bf16),
            pltpu.VMEM((rows, channels), bf16),
            pltpu.VMEM((rows, channels), bf16),
            pltpu.VMEM((rows, channels), bf16),
            pltpu.VMEM(conv_taps.shape, f32),
            pltpu.VMEM((1, channels), f32),
            pltpu.VMEM((1, lag_profile.shape[0]), f32),
            pltpu.VMEM((1, channels), f32),
            pltpu.VMEM(pairs.shape, jnp.int32),
            pltpu.VMEM((8, channels), f32),
            pltpu.VMEM((8, channels), f32),
            pltpu.VMEM(piece, bf16),
            pltpu.VMEM(piece, f32),
            pltpu.VMEM(piece, bf16),
            pltpu.VMEM((chunks, supers, rows, width), bf16),
            pltpu.VMEM((chunks, supers, wide, width), bf16),
            pltpu.VMEM((n // 2, wide, wide), bf16),
            pltpu.VMEM((chunks, boxed, wide, width), bf16),
            pltpu.VMEM((chunks, boxed, wide, width), bf16),
            pltpu.VMEM((chunks, supers, wide, width), f32),
            pltpu.VMEM(piece, bf16),
            pltpu.VMEM(piece, bf16),
            dma((8,)),
            dma((chunks, members)),
            dma((2,)),
            dma((chunks, members)),
            dma((chunks, members)),
            dma((chunks, members)),
            dma((chunks, members)),
            dma((chunks,)),
            dma((chunks,)),
        ],
        compiler_params=pltpu.CompilerParams(
            collective_id=0, has_side_effects=True, vmem_limit_bytes=62 * 1024 * 1024
        ),
    )(
        query_rows, key_rows, value_rows, conv_taps, decay_rate.reshape(1, -1),
        lag_profile.reshape(1, -1), skip_gain.reshape(1, -1), pairs,
    )
    return pl.pallas_call(
        functools.partial(hand_over, rows // STRIPS),
        out_shape=jax.ShapeDtypeStruct((rows, channels), bf16),
        in_specs=[hbm],
        out_specs=hbm,
        scratch_shapes=[pltpu.VMEM((rows, channels), bf16), dma((STRIPS,)), dma((STRIPS,))],
        compiler_params=pltpu.CompilerParams(vmem_limit_bytes=62 * 1024 * 1024),
    )(held)


def solution(mesh):
    rows = P(("group", "ctx"), None)
    return jax.shard_map(
        on_device,
        mesh=mesh,
        in_specs=(rows, rows, rows, P(), P(), P(), P(), P("group", None, None)),
        out_specs=rows,
        check_vma=False,
    )
```
